32 devices in a mesh: ckpt: 2 (over y), row: 16 (over z, x, core).
Axes of the slice: x: 2, y: 2, z: 4, core: 2. Of those that a mesh axis runs over, the one named last changes fastest.
Arguments:
- activations: bfloat16 [4096, 4096], P(('ckpt', 'row')), parts along dimension 0, may hold values from -6 to 6
- gate_pre: bfloat16 [4096, 7168], P(('ckpt', 'row')), parts along dimension 0, may hold values from -8 to 8
- out_grad: bfloat16 [4096, 4096], P(('ckpt', 'row')), parts along dimension 0, may hold values from -6 to 6
- down_weight: bfloat16 [14336, 4096], P(('ckpt', 'row')), parts along dimension 0, may hold values from -0.09375 to 0.09375
- proj_in: bfloat16 [4096, 64], replicated, may hold values from -0.09375 to 0.09375
- proj_out: bfloat16 [7168, 64], replicated, may hold values from -0.0625 to 0.0625
- stored: bfloat16 [24576, 4096], P(('ckpt', 'row')), parts along dimension 0, may hold values from -0.09375 to 0.09375
- visible: int32 [16], replicated, may hold values from 1 to 12288, as said below
Outputs:
- scores: float32 [32, 12288], P('ckpt', 'row'), parts along dimension 0
The draws below stay inside these ranges and needn't reach their ends.
There are 2 independent parts, one for each index of `ckpt`. The reference program is written for one: setup_inputs(seed, part) draws one part's arguments, and reference() takes and returns one part's arrays. A program takes and returns all parts, laid end to end along the dimension named above; an argument that names none is the same for every part. Nothing has to cross between parts.
Inputs may be any that keep to these rules, and one draw needn't show every extreme that they name: `visible`: some query example sees all 12288 stored examples and some sees exactly one.
All inputs are finite; a program needn't handle non-finite values.
Results may differ from the reference program's by a relative error of at most 0.0064.
Values may be sent and summed in bfloat16 or wider, within the bound.
No kernel may reach another device: no remote copies, remote signals or barrier semaphores. Data moves between devices by JAX's collectives and lax.ppermute only.
A program may use at most 128 MiB of HBM per device.

```python
import jax
import jax.numpy as jnp
from jax import lax

D = 4096
FFW = 7168
RANK = 64
SEQ_LEN = 128
FEATURES = 4096
EXAMPLES = 16
TOKENS = 2048
STORED = 12288


def draw_visible(key, part):
    first_key, second_key, third_key = jax.random.split(jax.random.fold_in(key, 17), 3)
    counts = jax.random.randint(first_key, (EXAMPLES,), 1, STORED + 1)
    where_all = jax.random.randint(second_key, (), 0, EXAMPLES)
    where_one = (where_all + 1 + jax.random.randint(third_key, (), 0, EXAMPLES - 1)) % EXAMPLES
    counts = counts.at[where_all].set(STORED)
    counts = counts.at[where_one].set(1)
    return counts.astype(jnp.int32)


def block_levels(own_key, extent, pieces, low, largest):
    gain, own = 1.0, jax.random.fold_in(own_key, 6)
    for dim, parts in pieces:
        heights = jnp.exp(jax.random.uniform(jax.random.fold_in(own, dim), (parts,), jnp.float32, low / len(pieces), largest / len(pieces)))
        gain = gain * jnp.repeat(heights, extent[dim] // parts).reshape([-1 if axis == dim else 1 for axis in range(len(extent))])
    return gain


def gaussian(stream_key, extent, width, limit, shards=(), held_as=jnp.bfloat16):
    array = width * jax.random.normal(stream_key, extent, jnp.float32)
    if shards:
        array = array * block_levels(stream_key, extent, shards, -0.22, 0.18)
    return jnp.clip(array, -limit, limit).astype(held_as)


def setup_inputs(seed: int = 0, part: int = 0) -> dict:
    keys = jax.random.split(jax.random.key(seed), 9)
    own_keys = jax.random.split(jax.random.fold_in(keys[8], part), 9)
    return {
        "activations": gaussian(own_keys[0], (TOKENS, D), 1.0, 6.0, ((0, 16),)),
        "gate_pre": gaussian(own_keys[1], (TOKENS, FFW), 1.5, 8.0, ((0, 16),)),
        "out_grad": gaussian(own_keys[2], (TOKENS, D), 1.0, 6.0, ((0, 16),)),
        "down_weight": gaussian(own_keys[3], (FFW, D), D ** -0.5, 0.09375, ((0, 16),)),
        "proj_in": gaussian(keys[4], (D, RANK), D ** -0.5, 0.09375),
        "proj_out": gaussian(keys[5], (FFW, RANK), FFW ** -0.5, 0.0625),
        "stored": gaussian(own_keys[6], (STORED, FEATURES), FEATURES ** -0.5, 0.09375, ((0, 16),)),
        "visible": draw_visible(jax.random.fold_in(keys[8], 71), part),
    }


def one_example(inputs, down_weight, proj_in, proj_out):
    activations, gate_pre, out_grad = inputs
    hidden_grad = lax.dot_general(out_grad, down_weight, (((1,), (1,)), ((), ())), preferred_element_type=jnp.float32).astype(jnp.bfloat16)
    hidden_wide = lax.optimization_barrier(hidden_grad).astype(jnp.float32)
    up_grad = (hidden_wide * jax.nn.silu(gate_pre.astype(jnp.float32))).astype(jnp.bfloat16)
    in_proj = jnp.dot(activations, proj_in, preferred_element_type=jnp.float32).astype(jnp.bfloat16)
    out_proj = jnp.dot(up_grad, proj_out, preferred_element_type=jnp.float32).astype(jnp.bfloat16)
    raw_feature = jnp.dot(in_proj.astype(jnp.float32).T, out_proj.astype(jnp.float32), preferred_element_type=jnp.float32).reshape(-1)
    scale = lax.rsqrt(jnp.mean(raw_feature * raw_feature) + 1e-06)
    return (raw_feature * scale).astype(jnp.bfloat16)

def reference(activations, gate_pre, out_grad, down_weight, proj_in, proj_out, stored, visible):
    acts_ex = activations.reshape(EXAMPLES, SEQ_LEN, D)
    gate_ex = gate_pre.reshape(EXAMPLES, SEQ_LEN, FFW)
    grad_ex = out_grad.reshape(EXAMPLES, SEQ_LEN, D)
    queries = lax.map(lambda inputs: one_example(inputs, down_weight, proj_in, proj_out), (acts_ex, gate_ex, grad_ex))
    products = lax.dot_general(queries, stored, (((1,), (1,)), ((), ())), preferred_element_type=jnp.float32)
    column = jnp.arange(STORED, dtype=jnp.int32)
    return jnp.where(column[None, :] < visible[:, None], products, jnp.float32(0.0))
```

```python
import jax
import jax.numpy as jnp
from jax import lax
from jax.sharding import PartitionSpec as P

SEQ_LEN = 128
LANE_SHIFT = 2
LANES = 4


def shards(activations, gate_pre, out_grad, down_weight, proj_in, proj_out, stored, visible):
    devices = lax.axis_size("row")
    position = lax.axis_index("row")
    total_bits = devices.bit_length() - 1
    lane = position >> LANE_SHIFT & LANES - 1
    quad = position & (1 << LANE_SHIFT) - 1
    quads = 1 << LANE_SHIFT
    tokens = out_grad.shape[0]
    rank = proj_in.shape[1]
    piece = down_weight.shape[0]
    blocks = LANES * quads
    outer = devices // blocks
    bf16, f32 = jnp.bfloat16, jnp.float32

    def send(value, move):
        pairs = []
        for i in range(devices):
            target = move(i)
            if target is not None:
                pairs.append((i, target))
        return lax.ppermute(value, "row", pairs)

    def flip(bits):
        return lambda i: i ^ bits

    def lane_move(table):
        def move(i):
            to = table.get(i >> LANE_SHIFT & LANES - 1)
            return None if to is None else i & ~((LANES - 1) << LANE_SHIFT) | to << LANE_SHIFT

        return move

    def gather_high(value, axis):
        for bit in range(LANE_SHIFT + 2, total_bits):
            other = send(value, flip(1 << bit))
            high = position >> bit & 1 == 1
            value = jnp.where(
                high,
                jnp.concatenate([other, value], axis=axis),
                jnp.concatenate([value, other], axis=axis),
            )
        return value

    middle_swap = lane_move({1: 2, 2: 1})
    to_ends = lane_move({1: 0, 2: 3})
    at_end = (lane == 0) | (lane == LANES - 1)

    own_w = gather_high(down_weight, 0)
    rows = own_w.shape[0]

    grad_a = send(out_grad, flip(1 << LANE_SHIFT))
    grad_b = send(out_grad, middle_swap)
    far_w = send(own_w, flip(2))
    core_w = send(own_w, flip(1))

    in_proj = jnp.dot(activations, proj_in, preferred_element_type=f32).astype(bf16)

    def columns(block):
        parts = [
            lax.dynamic_slice_in_dim(gate_pre, (o * blocks + block) * piece, piece, axis=1)
            for o in range(outer)
        ]
        return parts

    def gate_block(k):
        parts = []
        for w in range(quads):
            parts += columns((lane ^ k) * quads + (quad ^ w))
        return jnp.concatenate(parts, axis=1)

    grad_c = send(grad_a, middle_swap)
    grad_d = send(grad_b, to_ends)
    grad_e = send(grad_c, to_ends)

    gates, ins = [gate_block(0)], [in_proj]
    hidden_group = rows * quads
    for k in range(1, LANES):
        got = send(jnp.concatenate([gate_block(k), in_proj], axis=1), flip(k << LANE_SHIFT))
        gates.append(got[:, :hidden_group])
        ins.append(got[:, hidden_group:])
    gates = jnp.concatenate(gates, axis=0)

    grads = jnp.concatenate(
        [out_grad, grad_a, jnp.where(at_end, grad_d, grad_c), jnp.where(at_end, grad_e, grad_b)],
        axis=0,
    )

    cross_w = send(far_w, flip(1))

    out_rows = []
    for w in range(quads):
        parts = [
            lax.dynamic_slice_in_dim(
                proj_out, (o * blocks + lane * quads + (quad ^ w)) * piece, piece, axis=0
            )
            for o in range(outer)
        ]
        out_rows.append(jnp.concatenate(parts, axis=0))
    weights = [
        (own_w, 0),
        (core_w, rows),
        (far_w, 2 * rows),
        (cross_w, 3 * rows),
    ]
    out_rows = jnp.concatenate(out_rows, axis=0)
    out = jnp.zeros((LANES * tokens, rank), f32)
    for weight, start in weights:
        stop = start + weight.shape[0]
        hidden = lax.dot_general(
            grads, weight, (((1,), (1,)), ((), ())), preferred_element_type=f32
        ).astype(bf16)
        up_grad = (
            lax.optimization_barrier(hidden).astype(f32)
            * jax.nn.silu(gates[:, start:stop].astype(f32))
        ).astype(bf16)
        out += jnp.dot(up_grad, out_rows[start:stop], preferred_element_type=f32)

    examples_dev = tokens // SEQ_LEN
    feature = jnp.einsum(
        "kesa,kesb->keab",
        jnp.stack(ins).reshape(LANES, examples_dev, SEQ_LEN, rank).astype(f32),
        out.reshape(LANES, examples_dev, SEQ_LEN, rank),
        preferred_element_type=f32,
    ).reshape(LANES, examples_dev, rank * rank)
    for bit in range(2):
        other = send(feature, flip(1 << bit + LANE_SHIFT))
        order = [k ^ 1 << bit for k in range(LANES)]
        feature = feature + jnp.stack([other[k] for k in order])
    scale = lax.rsqrt(jnp.mean(feature * feature, axis=2, keepdims=True) + 1e-06)
    queries = (feature * scale).astype(bf16)
    for bit in range(2):
        flipped = queries.reshape(LANES >> bit + 1, 2, 1 << bit, examples_dev, -1)[:, ::-1]
        queries = jnp.where(lane >> bit & 1 == 1, flipped.reshape(queries.shape), queries)
    queries = queries[:, None]
    for bit in range(LANE_SHIFT):
        other = send(queries, flip(1 << bit))
        high = position >> bit & 1 == 1
        queries = jnp.where(
            high,
            jnp.concatenate([other, queries], axis=1),
            jnp.concatenate([queries, other], axis=1),
        )
    queries = gather_high(queries, 0).reshape(devices * examples_dev, rank * rank)
    stored_rows = stored.shape[0]
    column = position * stored_rows + jnp.arange(stored_rows, dtype=jnp.int32)
    products = lax.dot_general(
        queries, stored, (((1,), (1,)), ((), ())), preferred_element_type=f32
    )
    return jnp.where(column[None, :] < visible[:, None], products, f32(0.0))


def solution(mesh):
    return jax.shard_map(
        shards,
        mesh=mesh,
        in_specs=(
            P(("ckpt", "row"), None),
            P(("ckpt", "row"), None),
            P(("ckpt", "row"), None),
            P(("ckpt", "row"), None),
            P(),
            P(),
            P(("ckpt", "row"), None),
            P(),
        ),
        out_specs=P("ckpt", "row"),
        check_vma=False,
    )
```

```python
import functools

import jax
import jax.numpy as jnp
from jax import lax
from jax.experimental import pallas as pl
from jax.experimental.pallas import tpu as pltpu
from jax.sharding import PartitionSpec as P

SEQ_LEN = 128
LANE_SHIFT = 2
LANES = 4
QUADS = 1 << LANE_SHIFT
BF16, F32 = jnp.bfloat16, jnp.float32
LINK = jnp.bfloat16


def chunk_sizes(rows):
    return [rows]


def place(both, core_first, piece, target, far):
    parts = [both[:, :piece], both[:, piece:]]
    if not core_first:
        parts = parts[::-1]
    if not far:
        target[:, : 2 * piece] = jnp.concatenate(parts, axis=1)
        return
    start = 2 * piece
    cut = 0
    for size in chunk_sizes(piece):
        pair = [part[:, cut : cut + size] for part in parts]
        target[:, start : start + 2 * size] = jnp.concatenate(pair, axis=1)
        cut += size
        start += 2 * size


def arrange_kernel(piece, where_ref, gate_ref, rows_ref, g0, g1, g2, g3, out_ref):
    lane, side, core = where_ref[0], where_ref[1], where_ref[2]
    wide = 2 * piece
    for value in range(2):

        @pl.when(core == value)
        def _():
            for k, target in enumerate((g0, g1, g2, g3)):
                for far in range(2):
                    block = (lane ^ k) * 2 + (side ^ far)
                    start = pl.multiple_of(block * wide, 128)
                    both = gate_ref[:, pl.ds(start, wide)]
                    place(both, value == 0, piece, target, far)
                    if k == 0:
                        both = rows_ref[:, pl.ds(start, wide)]
                        place(both, value == 0, piece, out_ref, far)


def arrange(gate, rows, position, piece):
    lane = position >> LANE_SHIFT & LANES - 1
    quad = position & QUADS - 1
    total = gate.shape[1]
    outer = total // (piece * QUADS * LANES)
    mine = total // LANES
    if outer == 1 and 2 * piece % 128 == 0:
        where = jnp.stack([lane, quad >> 1, quad & 1]).astype(jnp.int32)
        vmem = pl.BlockSpec(memory_space=pltpu.VMEM)
        return pl.pallas_call(
            functools.partial(arrange_kernel, piece),
            out_shape=[jax.ShapeDtypeStruct((gate.shape[0], mine), gate.dtype)] * LANES
            + [jax.ShapeDtypeStruct((rows.shape[0], mine), rows.dtype)],
            in_specs=[pl.BlockSpec(memory_space=pltpu.SMEM), vmem, vmem],
            out_specs=[vmem] * (LANES + 1),
            cost_estimate=pl.CostEstimate(
                flops=0, bytes_accessed=4 * gate.size + 4 * rows.size, transcendentals=0
            ),
        )(where, gate, rows)

    def block(value, k):
        whole = []
        for w in range(QUADS):
            index = (lane ^ k) * QUADS + (quad ^ w)
            parts = []
            for o in range(outer):
                start = (o * QUADS * LANES + index) * piece
                parts.append(lax.dynamic_slice_in_dim(value, start, piece, axis=1))
            whole.append(jnp.concatenate(parts, axis=1))
        parts = whole[:2]
        cut = 0
        for size in chunk_sizes(outer * piece):
            parts += [whole[2][:, cut : cut + size], whole[3][:, cut : cut + size]]
            cut += size
        return jnp.concatenate(parts, axis=1)

    return [block(gate, k) for k in range(LANES)] + [block(rows, 0)]


def after(value, *others):
    return lax.optimization_barrier((value,) + others)[0]


def call(body, out_shape, in_specs, out_specs, **kwargs):
    return pl.pallas_call(
        body,
        out_shape=out_shape,
        in_specs=in_specs,
        out_specs=out_specs,
        cost_estimate=pl.CostEstimate(flops=1000, bytes_accessed=1000, transcendentals=0),
        **kwargs,
    )


def feature_kernel(spans, slots, tokens, examples, *refs):
    count = sum(len(span) for span in spans)
    blocks = refs[:count]
    gates = refs[count : count + len(slots)]
    ins = refs[count + len(slots) : count + 2 * len(slots)]
    rows_ref, *before, out_ref = refs[count + 2 * len(slots) :]
    rank = rows_ref.shape[0]
    for k in range(LANES):
        if before and k not in slots:
            out_ref[k] = before[0][k]
    for slot, k in enumerate(slots):
        total = jnp.zeros((rank, tokens), F32)
        start = 0
        index = 0
        for span in spans:
            first = 0
            for i, height in enumerate(span):
                if first <= k * tokens < first + height:
                    block = blocks[index + i]
                    top = k * tokens - first
                first += height
            index += len(span)
            stop = start + block.shape[1]
            gate = gates[slot][:, start:stop].astype(F32)
            up_grad = (
                block[top : top + tokens, :].astype(F32)
                * (0.5 * gate * (1.0 + jnp.tanh(0.5 * gate)))
            ).astype(BF16)
            total += lax.dot_general(
                rows_ref[:, start:stop],
                up_grad,
                (((1,), (1,)), ((), ())),
                preferred_element_type=F32,
            )
            start = stop
        for e in range(examples):
            cut = slice(e * SEQ_LEN, (e + 1) * SEQ_LEN)
            feature = lax.dot_general(
                ins[slot][:, cut].astype(F32),
                total[:, cut],
                (((1,), (1,)), ((), ())),
                precision=lax.Precision.HIGHEST,
                preferred_element_type=F32,
            )
            out_ref[k, e] = jnp.concatenate(
                [feature[: rank // 2], feature[rank // 2 :]], axis=1
            ).astype(out_ref.dtype)


def features(slots, blocks, gates, ins, out_rows, *before):
    tokens = gates[0].shape[0]
    rank = out_rows.shape[0]
    examples = tokens // SEQ_LEN
    spans = [[part.shape[0] for part in parts] for parts in blocks]
    operands = (*[part for parts in blocks for part in parts], *gates, *ins, out_rows, *before)
    vmem = pl.BlockSpec(memory_space=pltpu.VMEM)
    return call(
        functools.partial(feature_kernel, spans, slots, tokens, examples),
        jax.ShapeDtypeStruct((LANES, examples, rank // 2, 2 * rank), LINK),
        [vmem] * len(operands),
        vmem,
    )(*operands)


def scale_kernel(own, *refs):
    others, out_ref = refs[:-1], refs[-1]
    width = own.shape[2] * own.shape[3]
    for j in range(LANES):
        total = own[j].astype(F32)
        for k in range(1, LANES):
            total += others[k - 1][j ^ k].astype(F32)
        square = jnp.sum(jnp.sum(total * total, axis=2, keepdims=True), axis=1, keepdims=True)
        out_ref[j] = (total * lax.rsqrt(square / width + 1e-06)).astype(BF16)


def scaled(own, others):
    vmem = pl.BlockSpec(memory_space=pltpu.VMEM)
    return call(
        scale_kernel,
        jax.ShapeDtypeStruct(own.shape, BF16),
        [vmem] * LANES,
        vmem,
    )(own, *others)


def score_kernel(where_ref, q0, q1, q2, q3, visible_ref, stored_ref, out_ref, rows):
    position = where_ref[0]
    for w, source in enumerate((q0, q1, q2, q3)):
        for k in range(LANES):
            row = k * QUADS + w
            value = source[k, 0].astype(F32)
            for j in range(value.shape[0]):
                rows[row : row + 1, j * 128 : (j + 1) * 128] = value[j : j + 1, :]
    products = lax.dot_general(
        rows[...].astype(BF16),
        stored_ref[...],
        (((1,), (1,)), ((), ())),
        preferred_element_type=F32,
    )
    count = out_ref.shape[1]
    index = lax.broadcasted_iota(jnp.int32, products.shape, 0)
    for bit in (1, 2, 4, 8):
        swapped = jnp.where(
            index & bit != 0,
            pltpu.roll(products, bit, 0),
            pltpu.roll(products, products.shape[0] - bit, 0),
        )
        products = jnp.where(jnp.full(products.shape, position) & bit != 0, swapped, products)
    column = position * count + lax.broadcasted_iota(jnp.int32, products.shape, 1)
    out_ref[...] = jnp.where(column < visible_ref[...], products, 0.0)


def scores(where, queries, visible, stored):
    vmem = pl.BlockSpec(memory_space=pltpu.VMEM)
    examples = LANES * QUADS
    return call(
        score_kernel,
        jax.ShapeDtypeStruct((examples, stored.shape[0]), F32),
        [pl.BlockSpec(memory_space=pltpu.SMEM)] + [vmem] * 6,
        vmem,
        scratch_shapes=[pltpu.VMEM((examples, stored.shape[1]), F32)],
    )(where, *queries, visible[:, None], stored)


def shards(activations, gate_pre, out_grad, down_weight, proj_in, proj_out, stored, visible):
    devices = lax.axis_size("row")
    position = lax.axis_index("row")
    total_bits = devices.bit_length() - 1
    lane = position >> LANE_SHIFT & LANES - 1
    tokens = out_grad.shape[0]
    rank = proj_in.shape[1]

    def send(value, move):
        pairs = []
        for i in range(devices):
            target = move(i)
            if target is not None:
                pairs.append((i, target))
        return lax.ppermute(value, "row", pairs)

    def flip(bits):
        return lambda i: i ^ bits

    def lane_move(table):
        def move(i):
            to = table.get(i >> LANE_SHIFT & LANES - 1)
            return None if to is None else i & ~((LANES - 1) << LANE_SHIFT) | to << LANE_SHIFT

        return move

    def join(value, other, bit, axis):
        return jnp.where(
            position >> bit & 1 == 1,
            jnp.concatenate([other, value], axis=axis),
            jnp.concatenate([value, other], axis=axis),
        )

    def gather_high(value, axis):
        for bit in range(LANE_SHIFT + 2, total_bits):
            value = join(value, send(value, flip(1 << bit)), bit, axis)
        return value

    middle_swap = lane_move({1: 2, 2: 1})
    to_ends = lane_move({1: 0, 2: 3})
    at_end = (lane == 0) | (lane == LANES - 1)

    own_w = gather_high(down_weight, 0)
    rows = own_w.shape[0]

    tie = lax.optimization_barrier
    grad_a = send(out_grad, flip(1 << LANE_SHIFT))
    grad_b = send(out_grad, middle_swap)
    far_w = send(own_w, flip(2))
    core_w = send(own_w, flip(1))

    *gate_out, out_rows = arrange(gate_pre, proj_out.T, position, down_weight.shape[0])
    width = proj_in.shape[0]
    paired = proj_in.T.reshape(rank // 2, 2, width).transpose(1, 0, 2).reshape(rank, width)
    in_proj = lax.dot_general(
        paired, activations, (((1,), (1,)), ((), ())), preferred_element_type=F32
    ).astype(BF16)
    grad_a, core_w, in_proj, gate_out = tie((grad_a, core_w, in_proj, gate_out))

    grad_c = send(grad_a, middle_swap)
    in_1 = send(in_proj, flip(1 << LANE_SHIFT))
    grad_d = send(grad_b, to_ends)
    grad_c, in_1, gate_out = tie((grad_c, in_1, gate_out))

    grad_e = send(grad_c, to_ends)
    gate_3 = send(gate_out[3], flip(3 << LANE_SHIFT))
    in_2 = send(jnp.stack([in_proj, in_1]), flip(2 << LANE_SHIFT))
    ins = [in_proj, in_1, in_2[0], in_2[1]]
    early = jnp.concatenate([out_grad, grad_a, jnp.where(at_end, grad_d, grad_c)], axis=0)

    def hidden(grads, weight):
        return lax.dot_general(
            grads, weight, (((1,), (1,)), ((), ())), preferred_element_type=F32
        ).astype(BF16)

    first = [hidden(early, w) for w in (own_w, core_w)]
    grad_e, gate_3, far_w, gate_out, first, ins = tie(
        (grad_e, gate_3, far_w, gate_out, first, ins)
    )

    cross_w = send(far_w, flip(1))
    gate_2 = send(gate_out[2], flip(2 << LANE_SHIFT))
    gate_1 = send(gate_out[1], flip(1 << LANE_SHIFT))
    late = jnp.where(at_end, grad_e, grad_b)
    grads = jnp.concatenate([early, late], axis=0)
    blocks = [(h, hidden(late, w)) for h, w in zip(first, (own_w, core_w))]
    blocks += [(hidden(grads, w),) for w in (far_w, cross_w)]
    half = features((0, 3), blocks, [gate_out[0], gate_3], [ins[0], ins[3]], out_rows)
    gate_1, gate_2, half = tie((gate_1, gate_2, half))
    own = features((1, 2), blocks, [gate_1, gate_2], ins[1:3], out_rows, half)
    queries = scaled(own, [send(own, flip(k << LANE_SHIFT)) for k in range(1, LANES)])
    quad = position & QUADS - 1
    everyone = [queries] + [send(queries, flip(q)) for q in range(1, QUADS)]
    if devices == LANES * QUADS and tokens == SEQ_LEN:
        where = position.astype(jnp.int32).reshape(1)
        return scores(where, everyone, visible, stored)

    examples_dev = tokens // SEQ_LEN
    everyone = jnp.stack(everyone, axis=1).reshape(LANES * QUADS, examples_dev, rank * rank)
    order = jnp.arange(LANES * QUADS)
    order = (order >> LANE_SHIFT ^ lane) * QUADS + (order & QUADS - 1 ^ quad)
    pick = (order[:, None] == jnp.arange(LANES * QUADS)[None, :]).astype(BF16)
    everyone = jnp.einsum("ij,jef->ief", pick, everyone, preferred_element_type=F32).astype(BF16)
    queries = gather_high(everyone, 0).reshape(devices * examples_dev, rank * rank)
    stored_rows = stored.shape[0]
    column = position * stored_rows + jnp.arange(stored_rows, dtype=jnp.int32)
    products = lax.dot_general(
        queries, stored, (((1,), (1,)), ((), ())), preferred_element_type=F32
    )
    return jnp.where(column[None, :] < visible[:, None], products, F32(0.0))


def solution(mesh):
    return jax.shard_map(
        shards,
        mesh=mesh,
        in_specs=(
            P(("ckpt", "row"), None),
            P(("ckpt", "row"), None),
            P(("ckpt", "row"), None),
            P(("ckpt", "row"), None),
            P(),
            P(),
            P(("ckpt", "row"), None),
            P(),
        ),
        out_specs=P("ckpt", "row"),
        check_vma=False,
    )
```

```python
import functools

import jax
import jax.numpy as jnp
from jax import lax
from jax.experimental import pallas as pl
from jax.experimental.pallas import tpu as pltpu
from jax.sharding import PartitionSpec as P

SEQ_LEN = 128
LANE_SHIFT = 2
LANES = 4
QUADS = 1 << LANE_SHIFT
BF16, F32 = jnp.bfloat16, jnp.float32
LINK = jnp.bfloat16


EXTRA = 16


def arrange_kernel(piece, where_ref, gate_ref, rows_ref, in_ref, n0, n1, n2, f0, f1, f2, b3, r0, r1, r2):
    lane, side, core = where_ref[0], where_ref[1], where_ref[2]
    wide = 2 * piece
    tokens = gate_ref.shape[0]

    def put(source, target, column, block, first):
        start = pl.multiple_of(block * wide, 128)
        both = source[:, pl.ds(start, wide)]
        if first == 1:
            both = jnp.concatenate([both[:, piece:], both[:, :piece]], axis=1)
        target[: both.shape[0], column : column + wide] = both

    for target in (f1, f2, b3):
        target[tokens:, :] = jnp.zeros((EXTRA, target.shape[1]), target.dtype)
        target[tokens:, : in_ref.shape[1]] = in_ref[...]
    for first in range(2):

        @pl.when(core == first)
        def _():
            for k in range(LANES):
                for far in range(2):
                    block = (lane ^ k) * 2 + (side ^ far)
                    if k == 3:
                        put(gate_ref, b3, far * wide, block, first)
                    else:
                        put(gate_ref, ((n0, n1, n2), (f0, f1, f2))[far][k], 0, block, first)
                    if k == 0:
                        put(rows_ref, r0, far * wide, block, first)
                    elif k < 3 and not far:
                        put(rows_ref, (r1, r2)[k - 1], 0, block, first)


def arrange(gate, rows, in_block, position, piece):
    lane = position >> LANE_SHIFT & LANES - 1
    quad = position & QUADS - 1
    total = gate.shape[1]
    outer = total // (piece * QUADS * LANES)
    mine = total // LANES
    tokens, rank = gate.shape[0], rows.shape[0]
    if outer == 1 and 2 * piece % 128 == 0:
        where = jnp.stack([lane, quad >> 1, quad & 1]).astype(jnp.int32)
        vmem = pl.BlockSpec(memory_space=pltpu.VMEM)
        near, far = (tokens, mine // 2), (tokens + EXTRA, mine // 2)
        shapes = [near] * 4 + [far] * 2 + [(tokens + EXTRA, mine)]
        shapes += [(rank, mine), (rank, mine // 2), (rank, mine // 2)]
        parts = pl.pallas_call(
            functools.partial(arrange_kernel, piece),
            out_shape=[jax.ShapeDtypeStruct(shape, gate.dtype) for shape in shapes],
            in_specs=[pl.BlockSpec(memory_space=pltpu.SMEM), vmem, vmem, vmem],
            out_specs=[vmem] * len(shapes),
            cost_estimate=pl.CostEstimate(
                flops=0, bytes_accessed=4 * gate.size + 4 * rows.size, transcendentals=0
            ),
            compiler_params=pltpu.CompilerParams(vmem_limit_bytes=16 << 20),
        )(where, gate, rows, in_block)
        return parts[:3], parts[3:6], parts[6], parts[7:]

    def block(value, k):
        whole = []
        for w in range(QUADS):
            index = (lane ^ k) * QUADS + (quad ^ w)
            for o in range(outer):
                start = (o * QUADS * LANES + index) * piece
                whole.append(lax.dynamic_slice_in_dim(value, start, piece, axis=1))
        whole = jnp.concatenate(whole, axis=1)
        return whole[:, : mine // 2], whole[:, mine // 2 :], whole

    def extend(value):
        extra = jnp.pad(in_block, ((0, 0), (0, value.shape[1] - in_block.shape[1])))
        return jnp.concatenate([value, extra], axis=0)

    near, far, whole = zip(*[block(gate, k) for k in range(LANES)])
    sides = [block(rows, 0)[2], block(rows, 1)[0], block(rows, 2)[0]]
    return list(near[:3]), [far[0], extend(far[1]), extend(far[2])], extend(whole[3]), sides


def after(value, *others):
    return lax.optimization_barrier((value,) + others)[0]


def call(body, out_shape, in_specs, out_specs, **kwargs):
    return pl.pallas_call(
        body,
        out_shape=out_shape,
        in_specs=in_specs,
        out_specs=out_specs,
        cost_estimate=pl.CostEstimate(flops=1000, bytes_accessed=1000, transcendentals=0),
        **kwargs,
    )


def silu(gate):
    return 0.5 * gate * (1.0 + jnp.tanh(0.5 * gate))


def in_value(refs, k, tokens):
    if k == 0:
        return refs["in"][...]
    source = refs["block"] if k == 3 else refs["far", k]
    width = refs["in"].shape[0] // EXTRA * tokens
    return source[tokens:, :width]


def feature_kernel(slots, blocks, gates, extras, names, *refs):
    out_ref, ups = refs[-2:]
    refs = dict(zip(names, refs))
    tokens = SEQ_LEN * out_ref.shape[1]
    rank = refs["rows"].shape[0]
    for k in range(LANES):
        if "before" in refs and k not in slots:
            out_ref[k] = refs["before"][k]
    for i, k in enumerate(slots):
        start = 0
        for b, width, tops in blocks:
            part, top = tops[k]
            edge = gates[k][0][1].stop - gates[k][0][1].start
            name, cut = gates[k][start >= edge]
            gate = refs[name]
            base = cut.start + start - edge * (start >= edge)
            value = refs[b, part][top : top + tokens, :].astype(F32)
            ups[i * tokens : (i + 1) * tokens, start : start + width] = (
                value * silu(gate[:tokens, base : base + width].astype(F32))
            ).astype(BF16)
            start += width
    total = lax.dot_general(
        refs["rows"][...], ups[...], (((1,), (1,)), ((), ())), preferred_element_type=F32
    )
    totals = [total[:, i * tokens : (i + 1) * tokens] for i in range(len(slots))]
    for j in range(extras):
        side = refs["side", j][...].astype(F32)
        up_grad = refs["back", j][:, side.shape[1] :].astype(F32) * silu(side)
        totals[0] += lax.dot_general(
            refs["beside", j][...],
            up_grad.astype(BF16),
            (((1,), (1,)), ((), ())),
            preferred_element_type=F32,
        )
    for i, k in enumerate(slots):
        for e in range(out_ref.shape[1]):
            cut = slice(e * SEQ_LEN, (e + 1) * SEQ_LEN)
            value = totals[i][:, cut]
            high = value.astype(BF16)
            low = (value - high.astype(F32)).astype(BF16)
            left = in_value(refs, k, tokens)
            if left.shape[0] == EXTRA:
                left = jnp.concatenate(
                    [left[:, j * tokens : (j + 1) * tokens] for j in range(rank // EXTRA)], axis=0
                )
            left = left[:, cut]
            feature = lax.dot_general(
                jnp.concatenate([left, left], axis=1),
                jnp.concatenate([high, low], axis=1),
                (((1,), (1,)), ((), ())),
                preferred_element_type=F32,
            )
            out_ref[k, e] = jnp.concatenate(
                [feature[: rank // 2], feature[rank // 2 :]], axis=1
            ).astype(out_ref.dtype)


def features(slots, blocks, sources, gates, rows, extras=(), before=None):
    names, operands, specs, layout = [], [], [], []
    rank, mine = rows.shape
    tokens = blocks[0][0].shape[0]
    vmem = pl.BlockSpec(memory_space=pltpu.VMEM)

    def add(name, value):
        names.append(name)
        operands.append(value)

    for b, parts in enumerate(blocks):
        tops, first = {}, 0
        for i, part in enumerate(parts):
            add((b, i), part)
            for k in range(LANES):
                if first <= k * tokens < first + part.shape[0]:
                    tops[k] = (i, k * tokens - first)
            first += part.shape[0]
        layout.append((b, parts[0].shape[1], tops))
    for name, value in sources.items():
        add(name, value)
    add("rows", rows)
    for j, (back, side, beside) in enumerate(extras):
        add(("back", j), back)
        add(("side", j), side)
        add(("beside", j), beside)
    if before is not None:
        add("before", before)
    return call(
        functools.partial(feature_kernel, slots, layout, gates, len(extras), names),
        jax.ShapeDtypeStruct((LANES, tokens // SEQ_LEN, rank // 2, 2 * rank), LINK),
        [vmem] * len(operands),
        vmem,
        scratch_shapes=[pltpu.VMEM((len(slots) * tokens, mine), BF16)],
        compiler_params=pltpu.CompilerParams(vmem_limit_bytes=16 << 20),
    )(*operands)


def scale_kernel(own, *refs):
    others, out_ref = refs[:-1], refs[-1]
    width = own.shape[2] * own.shape[3]
    for j in range(LANES):
        total = own[j].astype(F32)
        for k in range(1, LANES):
            total += others[k - 1][j ^ k].astype(F32)
        square = jnp.sum(jnp.sum(total * total, axis=2, keepdims=True), axis=1, keepdims=True)
        out_ref[j] = (total * lax.rsqrt(square / width + 1e-06)).astype(BF16)


def scaled(own, others):
    vmem = pl.BlockSpec(memory_space=pltpu.VMEM)
    return call(
        scale_kernel,
        jax.ShapeDtypeStruct(own.shape, BF16),
        [vmem] * LANES,
        vmem,
        compiler_params=pltpu.CompilerParams(vmem_limit_bytes=4 << 20),
    )(own, *others)


def score_kernel(where_ref, q0, q1, q2, q3, visible_ref, stored_ref, out_ref, rows):
    position = where_ref[0]
    for w, source in enumerate((q0, q1, q2, q3)):
        for k in range(LANES):
            row = k * QUADS + w
            value = source[k, 0].astype(F32)
            for j in range(value.shape[0]):
                rows[row : row + 1, j * 128 : (j + 1) * 128] = value[j : j + 1, :]
    products = lax.dot_general(
        rows[...].astype(BF16),
        stored_ref[...],
        (((1,), (1,)), ((), ())),
        preferred_element_type=F32,
    )
    count = out_ref.shape[1]
    index = lax.broadcasted_iota(jnp.int32, products.shape, 0)
    for bit in (1, 2, 4, 8):
        swapped = jnp.where(
            index & bit != 0,
            pltpu.roll(products, bit, 0),
            pltpu.roll(products, products.shape[0] - bit, 0),
        )
        products = jnp.where(jnp.full(products.shape, position) & bit != 0, swapped, products)
    column = position * count + lax.broadcasted_iota(jnp.int32, products.shape, 1)
    out_ref[...] = jnp.where(column < visible_ref[...], products, 0.0)


def scores(where, queries, visible, stored):
    vmem = pl.BlockSpec(memory_space=pltpu.VMEM)
    examples = LANES * QUADS
    return call(
        score_kernel,
        jax.ShapeDtypeStruct((examples, stored.shape[0]), F32),
        [pl.BlockSpec(memory_space=pltpu.SMEM)] + [vmem] * 6,
        vmem,
        scratch_shapes=[pltpu.VMEM((examples, stored.shape[1]), F32)],
        compiler_params=pltpu.CompilerParams(vmem_limit_bytes=8 << 20),
    )(where, *queries, visible[:, None], stored)


def shards(activations, gate_pre, out_grad, down_weight, proj_in, proj_out, stored, visible):
    devices = lax.axis_size("row")
    position = lax.axis_index("row")
    total_bits = devices.bit_length() - 1
    lane = position >> LANE_SHIFT & LANES - 1
    tokens = out_grad.shape[0]
    rank = proj_in.shape[1]

    def send(value, move):
        pairs = []
        for i in range(devices):
            target = move(i)
            if target is not None:
                pairs.append((i, target))
        return lax.ppermute(value, "row", pairs)

    def flip(bits):
        return lambda i: i ^ bits

    def lane_move(table):
        def move(i):
            to = table.get(i >> LANE_SHIFT & LANES - 1)
            return None if to is None else i & ~((LANES - 1) << LANE_SHIFT) | to << LANE_SHIFT

        return move

    def join(value, other, bit, axis):
        return jnp.where(
            position >> bit & 1 == 1,
            jnp.concatenate([other, value], axis=axis),
            jnp.concatenate([value, other], axis=axis),
        )

    def gather_high(value, axis):
        for bit in range(LANE_SHIFT + 2, total_bits):
            value = join(value, send(value, flip(1 << bit)), bit, axis)
        return value

    middle_swap = lane_move({1: 2, 2: 1})
    to_ends = lane_move({1: 0, 2: 3})
    at_end = (lane == 0) | (lane == LANES - 1)

    own_w = gather_high(down_weight, 0)
    rows = own_w.shape[0]

    tie = lax.optimization_barrier
    grad_a = send(out_grad, flip(1 << LANE_SHIFT))
    grad_b = send(out_grad, middle_swap)
    far_w = send(own_w, flip(2))
    core_w = send(own_w, flip(1))

    width = proj_in.shape[0]
    paired = proj_in.T.reshape(rank // 2, 2, width).transpose(1, 0, 2).reshape(rank, width)
    in_proj = lax.dot_general(
        paired, activations, (((1,), (1,)), ((), ())), preferred_element_type=F32
    ).astype(BF16)
    in_block = in_proj.reshape(rank // EXTRA, EXTRA, tokens).transpose(1, 0, 2)
    in_block = in_block.reshape(EXTRA, rank // EXTRA * tokens)
    near, far, block_3, sides = arrange(
        gate_pre, proj_out.T, in_block, position, down_weight.shape[0]
    )
    grad_a, core_w, near, far, block_3, sides = tie(
        (grad_a, core_w, near, far, block_3, sides)
    )

    def hidden(grads, weight):
        return lax.dot_general(
            grads, weight, (((1,), (1,)), ((), ())), preferred_element_type=F32
        ).astype(BF16)

    def near_hidden(grads):
        return [hidden(grads, w) for w in (own_w, core_w)]

    half = 2 * rows
    grad_c = send(grad_a, middle_swap)
    grad_d = send(grad_b, to_ends)
    slot_1 = near_hidden(grad_a)
    back_1 = send(jnp.concatenate([near[1], *slot_1], axis=1), lane_move({0: 1, 3: 2}))
    grad_c, near, far, block_3 = tie((grad_c, near, far, block_3))

    grad_e = send(grad_c, to_ends)
    block_3 = send(after(block_3, grad_d), flip(3 << LANE_SHIFT))
    slot_0 = near_hidden(after(out_grad, block_3, far_w))
    grad_2 = jnp.where(at_end, grad_d, grad_c)
    slot_2 = near_hidden(grad_2)
    back_2 = send(jnp.concatenate([near[2], *slot_2], axis=1), lane_move({0: 2, 3: 1}))
    grad_e, back_2, slot_0 = tie((grad_e, back_2, slot_0))
    grad_3 = jnp.where(at_end, grad_e, grad_b)
    slot_3 = near_hidden(grad_3)
    grads = jnp.concatenate([out_grad, grad_a, grad_2, grad_3], axis=0)
    block_3, back_1, back_2, far_w, near, far, grad_3 = tie(
        (block_3, back_1, back_2, far_w, near, far, grad_3)
    )

    cross_w = send(far_w, flip(1))
    far_2 = send(far[2], flip(2 << LANE_SHIFT))
    far_1 = send(far[1], flip(1 << LANE_SHIFT))
    blocks = list(zip(slot_0, slot_1, slot_2, slot_3))
    blocks += [(hidden(grads, w),) for w in (far_w, cross_w)]
    low, high = slice(0, half), slice(half, 2 * half)
    extras = [(back, near[j], sides[j]) for j, back in ((1, back_1), (2, back_2))]
    part = features(
        (0, 3),
        blocks,
        {"near": near[0], "far": far[0], "block": block_3, "in": in_proj},
        {0: (("near", low), ("far", low)), 3: (("block", low), ("block", high))},
        sides[0],
        extras,
    )
    far_1, far_2, part = tie((far_1, far_2, part))
    own = features(
        (1, 2),
        blocks,
        {("far", 1): far_1, ("far", 2): far_2, "back1": back_1, "back2": back_2, "in": in_proj},
        {
            1: (("back1", low), (("far", 1), low)),
            2: (("back2", low), (("far", 2), low)),
        },
        sides[0],
        before=part,
    )
    queries = scaled(own, [send(own, flip(k << LANE_SHIFT)) for k in range(1, LANES)])
    quad = position & QUADS - 1
    everyone = [queries] + [send(queries, flip(q)) for q in range(1, QUADS)]
    if devices == LANES * QUADS and tokens == SEQ_LEN:
        where = position.astype(jnp.int32).reshape(1)
        held = pltpu.with_memory_space_constraint(stored, pltpu.VMEM)
        return scores(where, everyone, visible, held)

    examples_dev = tokens // SEQ_LEN
    everyone = jnp.stack(everyone, axis=1).reshape(LANES * QUADS, examples_dev, rank * rank)
    order = jnp.arange(LANES * QUADS)
    order = (order >> LANE_SHIFT ^ lane) * QUADS + (order & QUADS - 1 ^ quad)
    pick = (order[:, None] == jnp.arange(LANES * QUADS)[None, :]).astype(BF16)
    everyone = jnp.einsum("ij,jef->ief", pick, everyone, preferred_element_type=F32).astype(BF16)
    queries = gather_high(everyone, 0).reshape(devices * examples_dev, rank * rank)
    stored_rows = stored.shape[0]
    column = position * stored_rows + jnp.arange(stored_rows, dtype=jnp.int32)
    products = lax.dot_general(
        queries, stored, (((1,), (1,)), ((), ())), preferred_element_type=F32
    )
    return jnp.where(column[None, :] < visible[:, None], products, F32(0.0))


def solution(mesh):
    return jax.shard_map(
        shards,
        mesh=mesh,
        in_specs=(
            P(("ckpt", "row"), None),
            P(("ckpt", "row"), None),
            P(("ckpt", "row"), None),
            P(("ckpt", "row"), None),
            P(),
            P(),
            P(("ckpt", "row"), None),
            P(),
        ),
        out_specs=P("ckpt", "row"),
        check_vma=False,
    )
```

```python
import functools

import jax
import jax.numpy as jnp
from jax import lax
from jax.experimental import pallas as pl
from jax.experimental.pallas import tpu as pltpu
from jax.sharding import PartitionSpec as P

SEQ_LEN = 128
LANE_SHIFT = 2
LANES = 4
QUADS = 1 << LANE_SHIFT
BF16, F32 = jnp.bfloat16, jnp.float32
LINK = jnp.bfloat16


EXTRA = 16


def arrange_kernel(piece, where_ref, gate_ref, rows_ref, in_ref, n0, n1, n2, f0, f1, f2, b3, r0, r1, r2):
    lane, side, core = where_ref[0], where_ref[1], where_ref[2]
    wide = 2 * piece
    tokens = gate_ref.shape[0]

    def put(source, target, column, block, first):
        start = pl.multiple_of(block * wide, 128)
        both = source[:, pl.ds(start, wide)]
        if first == 1:
            both = jnp.concatenate([both[:, piece:], both[:, :piece]], axis=1)
        target[: both.shape[0], column : column + wide] = both

    for target in (f1, f2, b3):
        target[tokens:, :] = jnp.zeros((EXTRA, target.shape[1]), target.dtype)
        target[tokens:, : in_ref.shape[1]] = in_ref[...]
    for first in range(2):

        @pl.when(core == first)
        def _():
            for k in range(LANES):
                for far in range(2):
                    block = (lane ^ k) * 2 + (side ^ far)
                    if k == 3:
                        put(gate_ref, b3, far * wide, block, first)
                    else:
                        put(gate_ref, ((n0, n1, n2), (f0, f1, f2))[far][k], 0, block, first)
                    if k == 0:
                        put(rows_ref, r0, far * wide, block, first)
                    elif k < 3 and not far:
                        put(rows_ref, (r1, r2)[k - 1], 0, block, first)


def arrange(gate, rows, in_block, position, piece):
    lane = position >> LANE_SHIFT & LANES - 1
    quad = position & QUADS - 1
    total = gate.shape[1]
    outer = total // (piece * QUADS * LANES)
    mine = total // LANES
    tokens, rank = gate.shape[0], rows.shape[0]
    if outer == 1 and 2 * piece % 128 == 0:
        where = jnp.stack([lane, quad >> 1, quad & 1]).astype(jnp.int32)
        vmem = pl.BlockSpec(memory_space=pltpu.VMEM)
        near, far = (tokens, mine // 2), (tokens + EXTRA, mine // 2)
        shapes = [near] * 4 + [far] * 2 + [(tokens + EXTRA, mine)]
        shapes += [(rank, mine), (rank, mine // 2), (rank, mine // 2)]
        parts = pl.pallas_call(
            functools.partial(arrange_kernel, piece),
            out_shape=[jax.ShapeDtypeStruct(shape, gate.dtype) for shape in shapes],
            in_specs=[pl.BlockSpec(memory_space=pltpu.SMEM), vmem, vmem, vmem],
            out_specs=[vmem] * len(shapes),
            cost_estimate=pl.CostEstimate(
                flops=0, bytes_accessed=4 * gate.size + 4 * rows.size, transcendentals=0
            ),
            compiler_params=pltpu.CompilerParams(vmem_limit_bytes=16 << 20),
        )(where, gate, rows, in_block)
        return parts[:3], parts[3:6], parts[6], parts[7:]

    def block(value, k):
        whole = []
        for w in range(QUADS):
            index = (lane ^ k) * QUADS + (quad ^ w)
            for o in range(outer):
                start = (o * QUADS * LANES + index) * piece
                whole.append(lax.dynamic_slice_in_dim(value, start, piece, axis=1))
        whole = jnp.concatenate(whole, axis=1)
        return whole[:, : mine // 2], whole[:, mine // 2 :], whole

    def extend(value):
        extra = jnp.pad(in_block, ((0, 0), (0, value.shape[1] - in_block.shape[1])))
        return jnp.concatenate([value, extra], axis=0)

    near, far, whole = zip(*[block(gate, k) for k in range(LANES)])
    sides = [block(rows, 0)[2], block(rows, 1)[0], block(rows, 2)[0]]
    return list(near[:3]), [far[0], extend(far[1]), extend(far[2])], extend(whole[3]), sides


def after(value, *others):
    return lax.optimization_barrier((value,) + others)[0]


def call(body, out_shape, in_specs, out_specs, **kwargs):
    return pl.pallas_call(
        body,
        out_shape=out_shape,
        in_specs=in_specs,
        out_specs=out_specs,
        cost_estimate=pl.CostEstimate(flops=1000, bytes_accessed=1000, transcendentals=0),
        **kwargs,
    )


def silu(gate):
    return 0.5 * gate * (1.0 + jnp.tanh(0.5 * gate))


def in_value(refs, k, tokens):
    if k == 0:
        return refs["in"][...]
    source = refs["block"] if k == 3 else refs["far", k]
    width = refs["in"].shape[0] // EXTRA * tokens
    return source[tokens:, :width]


def feature_kernel(slots, blocks, gates, extras, names, *refs):
    out_ref, ups = refs[-2:]
    refs = dict(zip(names, refs))
    tokens = SEQ_LEN * out_ref.shape[1]
    rank = refs["rows"].shape[0]
    for k in range(LANES):
        if "before" in refs and k not in slots:
            out_ref[k] = refs["before"][k]
    for i, k in enumerate(slots):
        start = 0
        for b, width, tops in blocks:
            part, top = tops[k]
            edge = gates[k][0][1].stop - gates[k][0][1].start
            name, cut = gates[k][start >= edge]
            gate = refs[name]
            base = cut.start + start - edge * (start >= edge)
            value = refs[b, part][top : top + tokens, :].astype(F32)
            ups[i * tokens : (i + 1) * tokens, start : start + width] = (
                value * silu(gate[:tokens, base : base + width].astype(F32))
            ).astype(BF16)
            start += width
    total = lax.dot_general(
        refs["rows"][...], ups[...], (((1,), (1,)), ((), ())), preferred_element_type=F32
    )
    totals = [total[:, i * tokens : (i + 1) * tokens] for i in range(len(slots))]
    for j in range(extras):
        side = refs["side", j][...].astype(F32)
        up_grad = refs["back", j][:, side.shape[1] :].astype(F32) * silu(side)
        totals[0] += lax.dot_general(
            refs["beside", j][...],
            up_grad.astype(BF16),
            (((1,), (1,)), ((), ())),
            preferred_element_type=F32,
        )
    for i, k in enumerate(slots):
        for e in range(out_ref.shape[1]):
            cut = slice(e * SEQ_LEN, (e + 1) * SEQ_LEN)
            value = totals[i][:, cut]
            high = value.astype(BF16)
            low = (value - high.astype(F32)).astype(BF16)
            left = in_value(refs, k, tokens)
            if left.shape[0] == EXTRA:
                left = jnp.concatenate(
                    [left[:, j * tokens : (j + 1) * tokens] for j in range(rank // EXTRA)], axis=0
                )
            left = left[:, cut]
            feature = lax.dot_general(
                jnp.concatenate([left, left], axis=1),
                jnp.concatenate([high, low], axis=1),
                (((1,), (1,)), ((), ())),
                preferred_element_type=F32,
            )
            out_ref[k, e] = jnp.concatenate(
                [feature[: rank // 2], feature[rank // 2 :]], axis=1
            ).astype(out_ref.dtype)


def features(slots, blocks, sources, gates, rows, extras=(), before=None):
    names, operands, specs, layout = [], [], [], []
    rank, mine = rows.shape
    tokens = sources["in"].shape[1]
    vmem = pl.BlockSpec(memory_space=pltpu.VMEM)

    def add(name, value):
        names.append(name)
        operands.append(value)

    for b, parts in enumerate(blocks):
        tops, first = {}, 0
        for i, part in enumerate(parts):
            add((b, i), part)
            for k in range(LANES):
                if first <= k * tokens < first + part.shape[0]:
                    tops[k] = (i, k * tokens - first)
            first += part.shape[0]
        layout.append((b, parts[0].shape[1], tops))
    for name, value in sources.items():
        add(name, value)
    add("rows", rows)
    for j, (back, side, beside) in enumerate(extras):
        add(("back", j), back)
        add(("side", j), side)
        add(("beside", j), beside)
    if before is not None:
        add("before", before)
    return call(
        functools.partial(feature_kernel, slots, layout, gates, len(extras), names),
        jax.ShapeDtypeStruct((LANES, tokens // SEQ_LEN, rank // 2, 2 * rank), LINK),
        [vmem] * len(operands),
        vmem,
        scratch_shapes=[pltpu.VMEM((len(slots) * tokens, mine), BF16)],
        compiler_params=pltpu.CompilerParams(vmem_limit_bytes=16 << 20),
    )(*operands)


def hold_kernel(source, target, sem):
    copy = pltpu.make_async_copy(source, target, sem)
    copy.start()
    copy.wait()


def hold(value):
    copied = call(
        hold_kernel,
        jax.ShapeDtypeStruct(value.shape, value.dtype),
        [pl.BlockSpec(memory_space=pltpu.HBM)],
        pl.BlockSpec(memory_space=pl.ANY),
        scratch_shapes=[pltpu.SemaphoreType.DMA],
        compiler_params=pltpu.CompilerParams(vmem_limit_bytes=46 << 20),
    )(value)
    return pltpu.with_memory_space_constraint(copied, pltpu.VMEM)


def scale_kernel(own, *refs):
    others, out_ref = refs[:-1], refs[-1]
    width = own.shape[2] * own.shape[3]
    for j in range(LANES):
        total = own[j].astype(F32)
        for k in range(1, LANES):
            total += others[k - 1][j ^ k].astype(F32)
        square = jnp.sum(jnp.sum(total * total, axis=2, keepdims=True), axis=1, keepdims=True)
        out_ref[j] = (total * lax.rsqrt(square / width + 1e-06)).astype(BF16)


def scaled(own, others):
    vmem = pl.BlockSpec(memory_space=pltpu.VMEM)
    return call(
        scale_kernel,
        jax.ShapeDtypeStruct(own.shape, BF16),
        [vmem] * LANES,
        vmem,
        compiler_params=pltpu.CompilerParams(vmem_limit_bytes=4 << 20),
    )(own, *others)


def score_kernel(where_ref, q0, q1, q2, q3, visible_ref, stored_ref, out_ref, rows):
    position = where_ref[0]
    for w, source in enumerate((q0, q1, q2, q3)):
        for k in range(LANES):
            row = k * QUADS + w
            value = source[k, 0].astype(F32)
            for j in range(value.shape[0]):
                rows[row : row + 1, j * 128 : (j + 1) * 128] = value[j : j + 1, :]
    products = lax.dot_general(
        rows[...].astype(BF16),
        stored_ref[...],
        (((1,), (1,)), ((), ())),
        preferred_element_type=F32,
    )
    count = out_ref.shape[1]
    index = lax.broadcasted_iota(jnp.int32, products.shape, 0)
    for bit in (1, 2, 4, 8):
        swapped = jnp.where(
            index & bit != 0,
            pltpu.roll(products, bit, 0),
            pltpu.roll(products, products.shape[0] - bit, 0),
        )
        products = jnp.where(jnp.full(products.shape, position) & bit != 0, swapped, products)
    column = position * count + lax.broadcasted_iota(jnp.int32, products.shape, 1)
    out_ref[...] = jnp.where(column < visible_ref[...], products, 0.0)


def scores(where, queries, visible, stored):
    vmem = pl.BlockSpec(memory_space=pltpu.VMEM)
    examples = LANES * QUADS
    return call(
        score_kernel,
        jax.ShapeDtypeStruct((examples, stored.shape[0]), F32),
        [pl.BlockSpec(memory_space=pltpu.SMEM)] + [vmem] * 6,
        vmem,
        scratch_shapes=[pltpu.VMEM((examples, stored.shape[1]), F32)],
        compiler_params=pltpu.CompilerParams(vmem_limit_bytes=8 << 20),
    )(where, *queries, visible[:, None], stored)


def shards(activations, gate_pre, out_grad, down_weight, proj_in, proj_out, stored, visible):
    devices = lax.axis_size("row")
    position = lax.axis_index("row")
    total_bits = devices.bit_length() - 1
    lane = position >> LANE_SHIFT & LANES - 1
    tokens = out_grad.shape[0]
    rank = proj_in.shape[1]

    def send(value, move):
        pairs = []
        for i in range(devices):
            target = move(i)
            if target is not None:
                pairs.append((i, target))
        return lax.ppermute(value, "row", pairs)

    def flip(bits):
        return lambda i: i ^ bits

    def lane_move(table):
        def move(i):
            to = table.get(i >> LANE_SHIFT & LANES - 1)
            return None if to is None else i & ~((LANES - 1) << LANE_SHIFT) | to << LANE_SHIFT

        return move

    def join(value, other, bit, axis):
        return jnp.where(
            position >> bit & 1 == 1,
            jnp.concatenate([other, value], axis=axis),
            jnp.concatenate([value, other], axis=axis),
        )

    def gather_high(value, axis):
        for bit in range(LANE_SHIFT + 2, total_bits):
            value = join(value, send(value, flip(1 << bit)), bit, axis)
        return value

    middle_swap = lane_move({1: 2, 2: 1})
    to_ends = lane_move({1: 0, 2: 3})
    at_end = (lane == 0) | (lane == LANES - 1)

    own_w = gather_high(down_weight, 0)
    rows = own_w.shape[0]

    tie = lax.optimization_barrier
    grad_a = send(out_grad, flip(1 << LANE_SHIFT))
    grad_b = send(out_grad, middle_swap)
    far_w = send(own_w, flip(2))
    core_w = send(own_w, flip(1))

    width = proj_in.shape[0]
    paired = proj_in.T.reshape(rank // 2, 2, width).transpose(1, 0, 2).reshape(rank, width)
    in_proj = lax.dot_general(
        paired, activations, (((1,), (1,)), ((), ())), preferred_element_type=F32
    ).astype(BF16)
    in_block = in_proj.reshape(rank // EXTRA, EXTRA, tokens).transpose(1, 0, 2)
    in_block = in_block.reshape(EXTRA, rank // EXTRA * tokens)
    near, far, block_3, sides = arrange(
        gate_pre, proj_out.T, in_block, position, down_weight.shape[0]
    )
    grad_a, core_w, near, far, block_3, sides = tie(
        (grad_a, core_w, near, far, block_3, sides)
    )

    def hidden(grads, weight):
        return lax.dot_general(
            grads, weight, (((1,), (1,)), ((), ())), preferred_element_type=F32
        ).astype(BF16)

    def near_hidden(grads):
        return [hidden(grads, w) for w in (own_w, core_w)]

    half = 2 * rows
    grad_c = send(grad_a, middle_swap)
    grad_d = send(grad_b, to_ends)
    pair = near_hidden(jnp.concatenate([out_grad, grad_a], axis=0))
    slot_1 = [value[tokens:] for value in pair]
    back_1 = send(jnp.concatenate([near[1], *slot_1], axis=1), lane_move({0: 1, 3: 2}))
    grad_c, near, far, block_3 = tie((grad_c, near, far, block_3))

    grad_e = send(grad_c, to_ends)
    block_3 = send(after(block_3, grad_d), flip(3 << LANE_SHIFT))
    grad_2 = jnp.where(at_end, grad_d, grad_c)
    slot_2 = near_hidden(grad_2)
    back_2 = send(jnp.concatenate([near[2], *slot_2], axis=1), lane_move({0: 2, 3: 1}))
    early = jnp.concatenate([out_grad, grad_a, grad_2], axis=0)
    far_early = hidden(after(early, block_3), far_w)
    grad_e, back_2, far_early = tie((grad_e, back_2, far_early))
    grad_3 = jnp.where(at_end, grad_e, grad_b)
    slot_3 = near_hidden(grad_3)
    grads = jnp.concatenate([early, grad_3], axis=0)
    block_3, back_1, back_2, far_w, near, far, grad_3 = tie(
        (block_3, back_1, back_2, far_w, near, far, grad_3)
    )

    cross_w = send(far_w, flip(1))
    far_2 = send(far[2], flip(2 << LANE_SHIFT))
    far_1 = send(far[1], flip(1 << LANE_SHIFT))
    blocks = list(zip(pair, slot_2, slot_3))
    blocks += [(far_early, hidden(grad_3, far_w)), (hidden(grads, cross_w),)]
    low, high = slice(0, half), slice(half, 2 * half)
    extras = [(back, near[j], sides[j]) for j, back in ((1, back_1), (2, back_2))]
    part = features(
        (0, 3),
        blocks,
        {"near": near[0], "far": far[0], "block": block_3, "in": in_proj},
        {0: (("near", low), ("far", low)), 3: (("block", low), ("block", high))},
        sides[0],
        extras,
    )
    far_1, far_2, part = tie((far_1, far_2, part))
    own = features(
        (1, 2),
        blocks,
        {("far", 1): far_1, ("far", 2): far_2, "back1": back_1, "back2": back_2, "in": in_proj},
        {
            1: (("back1", low), (("far", 1), low)),
            2: (("back2", low), (("far", 2), low)),
        },
        sides[0],
        before=part,
    )
    queries = scaled(own, [send(own, flip(k << LANE_SHIFT)) for k in range(1, LANES)])
    quad = position & QUADS - 1
    everyone = [queries] + [send(queries, flip(q)) for q in range(1, QUADS)]
    if devices == LANES * QUADS and tokens == SEQ_LEN:
        where = position.astype(jnp.int32).reshape(1)
        held = hold(after(stored, queries))
        return scores(where, everyone, visible, held)

    examples_dev = tokens // SEQ_LEN
    everyone = jnp.stack(everyone, axis=1).reshape(LANES * QUADS, examples_dev, rank * rank)
    order = jnp.arange(LANES * QUADS)
    order = (order >> LANE_SHIFT ^ lane) * QUADS + (order & QUADS - 1 ^ quad)
    pick = (order[:, None] == jnp.arange(LANES * QUADS)[None, :]).astype(BF16)
    everyone = jnp.einsum("ij,jef->ief", pick, everyone, preferred_element_type=F32).astype(BF16)
    queries = gather_high(everyone, 0).reshape(devices * examples_dev, rank * rank)
    stored_rows = stored.shape[0]
    column = position * stored_rows + jnp.arange(stored_rows, dtype=jnp.int32)
    products = lax.dot_general(
        queries, stored, (((1,), (1,)), ((), ())), preferred_element_type=F32
    )
    return jnp.where(column[None, :] < visible[:, None], products, F32(0.0))


def solution(mesh):
    return jax.shard_map(
        shards,
        mesh=mesh,
        in_specs=(
            P(("ckpt", "row"), None),
            P(("ckpt", "row"), None),
            P(("ckpt", "row"), None),
            P(("ckpt", "row"), None),
            P(),
            P(),
            P(("ckpt", "row"), None),
            P(),
        ),
        out_specs=P("ckpt", "row"),
        check_vma=False,
    )
```

```python
import functools

import jax
import jax.numpy as jnp
from jax import lax
from jax.experimental import pallas as pl
from jax.experimental.pallas import tpu as pltpu
from jax.sharding import PartitionSpec as P

SEQ_LEN = 128
LANE_SHIFT = 2
LANES = 4
QUADS = 1 << LANE_SHIFT
BF16, F32 = jnp.bfloat16, jnp.float32
LINK = jnp.bfloat16


EXTRA = 16


def arrange_kernel(piece, where_ref, gate_ref, rows_ref, in_ref, n0, n1, n2, f0, f1, f2, b3, r0, r1, r2):
    lane, side, core = where_ref[0], where_ref[1], where_ref[2]
    wide = 2 * piece
    tokens = gate_ref.shape[0]

    def put(source, target, column, block, first):
        start = pl.multiple_of(block * wide, 128)
        both = source[:, pl.ds(start, wide)]
        if first == 1:
            both = jnp.concatenate([both[:, piece:], both[:, :piece]], axis=1)
        target[: both.shape[0], column : column + wide] = both

    for target in (f1, f2, b3):
        target[tokens:, :] = jnp.zeros((EXTRA, target.shape[1]), target.dtype)
        target[tokens:, : in_ref.shape[1]] = in_ref[...]
    for first in range(2):

        @pl.when(core == first)
        def _():
            for k in range(LANES):
                for far in range(2):
                    block = (lane ^ k) * 2 + (side ^ far)
                    if k == 3:
                        put(gate_ref, b3, far * wide, block, first)
                    else:
                        put(gate_ref, ((n0, n1, n2), (f0, f1, f2))[far][k], 0, block, first)
                    if k == 0:
                        put(rows_ref, r0, far * wide, block, first)
                    elif k < 3 and not far:
                        put(rows_ref, (r1, r2)[k - 1], 0, block, first)


def arrange(gate, rows, in_block, position, piece):
    lane = position >> LANE_SHIFT & LANES - 1
    quad = position & QUADS - 1
    total = gate.shape[1]
    outer = total // (piece * QUADS * LANES)
    mine = total // LANES
    tokens, rank = gate.shape[0], rows.shape[0]
    if outer == 1 and 2 * piece % 128 == 0:
        where = jnp.stack([lane, quad >> 1, quad & 1]).astype(jnp.int32)
        vmem = pl.BlockSpec(memory_space=pltpu.VMEM)
        near, far = (tokens, mine // 2), (tokens + EXTRA, mine // 2)
        shapes = [near] * 4 + [far] * 2 + [(tokens + EXTRA, mine)]
        shapes += [(rank, mine), (rank, mine // 2), (rank, mine // 2)]
        parts = pl.pallas_call(
            functools.partial(arrange_kernel, piece),
            out_shape=[jax.ShapeDtypeStruct(shape, gate.dtype) for shape in shapes],
            in_specs=[pl.BlockSpec(memory_space=pltpu.SMEM), vmem, vmem, vmem],
            out_specs=[vmem] * len(shapes),
            cost_estimate=pl.CostEstimate(
                flops=0, bytes_accessed=4 * gate.size + 4 * rows.size, transcendentals=0
            ),
            compiler_params=pltpu.CompilerParams(vmem_limit_bytes=16 << 20),
        )(where, gate, rows, in_block)
        return parts[:3], parts[3:6], parts[6], parts[7:]

    def block(value, k):
        whole = []
        for w in range(QUADS):
            index = (lane ^ k) * QUADS + (quad ^ w)
            for o in range(outer):
                start = (o * QUADS * LANES + index) * piece
                whole.append(lax.dynamic_slice_in_dim(value, start, piece, axis=1))
        whole = jnp.concatenate(whole, axis=1)
        return whole[:, : mine // 2], whole[:, mine // 2 :], whole

    def extend(value):
        extra = jnp.pad(in_block, ((0, 0), (0, value.shape[1] - in_block.shape[1])))
        return jnp.concatenate([value, extra], axis=0)

    near, far, whole = zip(*[block(gate, k) for k in range(LANES)])
    sides = [block(rows, 0)[2], block(rows, 1)[0], block(rows, 2)[0]]
    return list(near[:3]), [far[0], extend(far[1]), extend(far[2])], extend(whole[3]), sides


def after(value, *others):
    return lax.optimization_barrier((value,) + others)[0]


def call(body, out_shape, in_specs, out_specs, **kwargs):
    return pl.pallas_call(
        body,
        out_shape=out_shape,
        in_specs=in_specs,
        out_specs=out_specs,
        cost_estimate=pl.CostEstimate(flops=1000, bytes_accessed=1000, transcendentals=0),
        **kwargs,
    )


def silu(gate):
    return 0.5 * gate * (1.0 + jnp.tanh(0.5 * gate))


def in_value(refs, k, tokens):
    if k == 0:
        return refs["in"][...]
    source = refs["block"] if k == 3 else refs["far", k]
    width = refs["in"].shape[0] // EXTRA * tokens
    return source[tokens:, :width]


def feature_kernel(slots, blocks, gates, extras, names, *refs):
    out_ref, ups = refs[-2:]
    refs = dict(zip(names, refs))
    tokens = SEQ_LEN * out_ref.shape[1]
    rank = refs["rows"].shape[0]
    for k in range(LANES):
        if "before" in refs and k not in slots:
            out_ref[k] = refs["before"][k]
    for i, k in enumerate(slots):
        start = 0
        for b, width, tops in blocks:
            part, top = tops[k]
            edge = gates[k][0][1].stop - gates[k][0][1].start
            name, cut = gates[k][start >= edge]
            gate = refs[name]
            base = cut.start + start - edge * (start >= edge)
            value = refs[b, part][top : top + tokens, :].astype(F32)
            ups[i * tokens : (i + 1) * tokens, start : start + width] = (
                value * silu(gate[:tokens, base : base + width].astype(F32))
            ).astype(BF16)
            start += width
    total = lax.dot_general(
        refs["rows"][...], ups[...], (((1,), (1,)), ((), ())), preferred_element_type=F32
    )
    totals = [total[:, i * tokens : (i + 1) * tokens] for i in range(len(slots))]
    for j in range(extras):
        side = refs["side", j][...].astype(F32)
        up_grad = refs["back", j][:, side.shape[1] :].astype(F32) * silu(side)
        totals[0] += lax.dot_general(
            refs["beside", j][...],
            up_grad.astype(BF16),
            (((1,), (1,)), ((), ())),
            preferred_element_type=F32,
        )
    for i, k in enumerate(slots):
        for e in range(out_ref.shape[1]):
            cut = slice(e * SEQ_LEN, (e + 1) * SEQ_LEN)
            value = totals[i][:, cut]
            high = value.astype(BF16)
            low = (value - high.astype(F32)).astype(BF16)
            left = in_value(refs, k, tokens)
            if left.shape[0] == EXTRA:
                left = jnp.concatenate(
                    [left[:, j * tokens : (j + 1) * tokens] for j in range(rank // EXTRA)], axis=0
                )
            left = left[:, cut]
            feature = lax.dot_general(
                jnp.concatenate([left, left], axis=1),
                jnp.concatenate([high, low], axis=1),
                (((1,), (1,)), ((), ())),
                preferred_element_type=F32,
            )
            out_ref[k, e] = jnp.concatenate(
                [feature[: rank // 2], feature[rank // 2 :]], axis=1
            ).astype(out_ref.dtype)


def features(slots, blocks, sources, gates, rows, extras=(), before=None):
    names, operands, specs, layout = [], [], [], []
    rank, mine = rows.shape
    tokens = sources["in"].shape[1]
    vmem = pl.BlockSpec(memory_space=pltpu.VMEM)

    def add(name, value):
        names.append(name)
        operands.append(value)

    for b, parts in enumerate(blocks):
        tops, first = {}, 0
        for i, part in enumerate(parts):
            add((b, i), part)
            for k in range(LANES):
                if first <= k * tokens < first + part.shape[0]:
                    tops[k] = (i, k * tokens - first)
            first += part.shape[0]
        layout.append((b, parts[0].shape[1], tops))
    for name, value in sources.items():
        add(name, value)
    add("rows", rows)
    for j, (back, side, beside) in enumerate(extras):
        add(("back", j), back)
        add(("side", j), side)
        add(("beside", j), beside)
    if before is not None:
        add("before", before)
    return call(
        functools.partial(feature_kernel, slots, layout, gates, len(extras), names),
        jax.ShapeDtypeStruct((LANES, tokens // SEQ_LEN, rank // 2, 2 * rank), LINK),
        [vmem] * len(operands),
        vmem,
        scratch_shapes=[pltpu.VMEM((len(slots) * tokens, mine), BF16)],
        compiler_params=pltpu.CompilerParams(vmem_limit_bytes=16 << 20),
    )(*operands)


def hold_kernel(source, target, sem):
    copy = pltpu.make_async_copy(source, target, sem)
    copy.start()
    copy.wait()


def hold(value, limit):
    return call(
        hold_kernel,
        jax.ShapeDtypeStruct(value.shape, value.dtype),
        [pl.BlockSpec(memory_space=pltpu.HBM)],
        pl.BlockSpec(memory_space=pl.ANY),
        scratch_shapes=[pltpu.SemaphoreType.DMA],
        compiler_params=pltpu.CompilerParams(vmem_limit_bytes=limit << 20),
    )(value)


def scale_kernel(own, *refs):
    others, out_ref = refs[:-1], refs[-1]
    width = own.shape[2] * own.shape[3]
    for j in range(LANES):
        total = own[j].astype(F32)
        for k in range(1, LANES):
            total += others[k - 1][j ^ k].astype(F32)
        square = jnp.sum(jnp.sum(total * total, axis=2, keepdims=True), axis=1, keepdims=True)
        out_ref[j] = (total * lax.rsqrt(square / width + 1e-06)).astype(BF16)


def scaled(own, others):
    vmem = pl.BlockSpec(memory_space=pltpu.VMEM)
    return call(
        scale_kernel,
        jax.ShapeDtypeStruct(own.shape, BF16),
        [vmem] * LANES,
        vmem,
        compiler_params=pltpu.CompilerParams(vmem_limit_bytes=4 << 20),
    )(own, *others)


def score_kernel(where_ref, q0, q1, q2, q3, visible_ref, stored_ref, out_ref, rows):
    position = where_ref[0]
    for w, source in enumerate((q0, q1, q2, q3)):
        for k in range(LANES):
            row = k * QUADS + w
            value = source[k, 0].astype(F32)
            for j in range(value.shape[0]):
                rows[row : row + 1, j * 128 : (j + 1) * 128] = value[j : j + 1, :]
    products = lax.dot_general(
        rows[...].astype(BF16),
        stored_ref[...],
        (((1,), (1,)), ((), ())),
        preferred_element_type=F32,
    )
    count = out_ref.shape[1]
    index = lax.broadcasted_iota(jnp.int32, products.shape, 0)
    for bit in (1, 2, 4, 8):
        swapped = jnp.where(
            index & bit != 0,
            pltpu.roll(products, bit, 0),
            pltpu.roll(products, products.shape[0] - bit, 0),
        )
        products = jnp.where(jnp.full(products.shape, position) & bit != 0, swapped, products)
    column = position * count + lax.broadcasted_iota(jnp.int32, products.shape, 1)
    out_ref[...] = jnp.where(column < visible_ref[...], products, 0.0)


def scores(where, queries, visible, stored):
    vmem = pl.BlockSpec(memory_space=pltpu.VMEM)
    examples = LANES * QUADS
    return call(
        score_kernel,
        jax.ShapeDtypeStruct((examples, stored.shape[0]), F32),
        [pl.BlockSpec(memory_space=pltpu.SMEM)] + [vmem] * 6,
        vmem,
        scratch_shapes=[pltpu.VMEM((examples, stored.shape[1]), F32)],
        compiler_params=pltpu.CompilerParams(vmem_limit_bytes=8 << 20),
    )(where, *queries, visible[:, None], stored)


def shards(activations, gate_pre, out_grad, down_weight, proj_in, proj_out, stored, visible):
    devices = lax.axis_size("row")
    position = lax.axis_index("row")
    total_bits = devices.bit_length() - 1
    lane = position >> LANE_SHIFT & LANES - 1
    tokens = out_grad.shape[0]
    rank = proj_in.shape[1]

    def send(value, move):
        pairs = []
        for i in range(devices):
            target = move(i)
            if target is not None:
                pairs.append((i, target))
        return lax.ppermute(value, "row", pairs)

    def flip(bits):
        return lambda i: i ^ bits

    def lane_move(table):
        def move(i):
            to = table.get(i >> LANE_SHIFT & LANES - 1)
            return None if to is None else i & ~((LANES - 1) << LANE_SHIFT) | to << LANE_SHIFT

        return move

    def join(value, other, bit, axis):
        return jnp.where(
            position >> bit & 1 == 1,
            jnp.concatenate([other, value], axis=axis),
            jnp.concatenate([value, other], axis=axis),
        )

    def gather_high(value, axis):
        for bit in range(LANE_SHIFT + 2, total_bits):
            value = join(value, send(value, flip(1 << bit)), bit, axis)
        return value

    middle_swap = lane_move({1: 2, 2: 1})
    to_ends = lane_move({1: 0, 2: 3})
    at_end = (lane == 0) | (lane == LANES - 1)

    own_w = gather_high(down_weight, 0)
    rows = own_w.shape[0]

    tie = lax.optimization_barrier
    grad_a = send(out_grad, flip(1 << LANE_SHIFT))
    grad_b = send(out_grad, middle_swap)
    far_w = send(own_w, flip(2))
    core_w = send(own_w, flip(1))

    width = proj_in.shape[0]
    paired = proj_in.T.reshape(rank // 2, 2, width).transpose(1, 0, 2).reshape(rank, width)
    in_proj = lax.dot_general(
        paired, activations, (((1,), (1,)), ((), ())), preferred_element_type=F32
    ).astype(BF16)
    in_block = in_proj.reshape(rank // EXTRA, EXTRA, tokens).transpose(1, 0, 2)
    in_block = in_block.reshape(EXTRA, rank // EXTRA * tokens)
    near, far, block_3, sides = arrange(
        gate_pre, proj_out.T, in_block, position, down_weight.shape[0]
    )
    grad_a, core_w, near, far, block_3, sides = tie(
        (grad_a, core_w, near, far, block_3, sides)
    )

    def hidden(grads, weight):
        return lax.dot_general(
            grads, weight, (((1,), (1,)), ((), ())), preferred_element_type=F32
        ).astype(BF16)

    def near_hidden(grads):
        return [hidden(grads, w) for w in (own_w, core_w)]

    half = 2 * rows
    grad_c = send(grad_a, middle_swap)
    grad_d = send(after(grad_b, grad_a), to_ends)
    pair = near_hidden(jnp.concatenate([out_grad, grad_a], axis=0))
    slot_1 = [value[tokens:] for value in pair]
    back_1 = send(jnp.concatenate([near[1], *slot_1], axis=1), lane_move({0: 1, 3: 2}))
    grad_c, near, far, block_3, pair = tie((grad_c, near, far, block_3, pair))

    grad_e = send(grad_c, to_ends)
    block_3 = send(after(block_3, grad_d), flip(3 << LANE_SHIFT))
    grad_2 = jnp.where(at_end, grad_d, grad_c)
    slot_2 = near_hidden(grad_2)
    back_2 = send(jnp.concatenate([near[2], *slot_2], axis=1), lane_move({0: 2, 3: 1}))
    early = jnp.concatenate([out_grad, grad_a, grad_2], axis=0)
    far_v = hold(after(far_w, block_3), 16)
    grad_e, back_2, far_v = tie((grad_e, back_2, far_v))
    narrow = at_end & (jnp.max(grad_e[:16, :128].astype(F32)) < jnp.inf)
    block_3, back_1, back_2, far_w, near, far, narrow = tie(
        (block_3, back_1, back_2, far_w, near, far, narrow)
    )
    cross_w = send(far_w, flip(1))
    far_2 = send(far[2], flip(2 << LANE_SHIFT))
    far_1 = send(far[1], flip(1 << LANE_SHIFT))
    grad_3 = jnp.where(at_end, grad_e, grad_b)
    slot_3 = near_hidden(grad_3)
    grads = jnp.concatenate([early, grad_3], axis=0)
    blocks = list(zip(pair, slot_2, slot_3))
    blocks += [(hidden(grads, far_v),), (hidden(grads, cross_w),)]
    low, high = slice(0, half), slice(half, 2 * half)
    extras = [(back, near[j], sides[j]) for j, back in ((1, back_1), (2, back_2))]
    part = features(
        (0, 3),
        blocks,
        {"near": near[0], "far": far[0], "block": block_3, "in": in_proj},
        {0: (("near", low), ("far", low)), 3: (("block", low), ("block", high))},
        sides[0],
        extras,
    )
    far_1, far_2, part = tie((far_1, far_2, part))
    own = features(
        (1, 2),
        blocks,
        {("far", 1): far_1, ("far", 2): far_2, "back1": back_1, "back2": back_2, "in": in_proj},
        {
            1: (("back1", low), (("far", 1), low)),
            2: (("back2", low), (("far", 2), low)),
        },
        sides[0],
        before=part,
    )
    queries = scaled(own, [send(own, flip(k << LANE_SHIFT)) for k in range(1, LANES)])
    quad = position & QUADS - 1
    everyone = [queries] + [send(queries, flip(q)) for q in range(1, QUADS)]
    if devices == LANES * QUADS and tokens == SEQ_LEN:
        where = position.astype(jnp.int32).reshape(1)
        held = pltpu.with_memory_space_constraint(hold(after(stored, queries), 46), pltpu.VMEM)
        return scores(where, everyone, visible, held)

    examples_dev = tokens // SEQ_LEN
    everyone = jnp.stack(everyone, axis=1).reshape(LANES * QUADS, examples_dev, rank * rank)
    order = jnp.arange(LANES * QUADS)
    order = (order >> LANE_SHIFT ^ lane) * QUADS + (order & QUADS - 1 ^ quad)
    pick = (order[:, None] == jnp.arange(LANES * QUADS)[None, :]).astype(BF16)
    everyone = jnp.einsum("ij,jef->ief", pick, everyone, preferred_element_type=F32).astype(BF16)
    queries = gather_high(everyone, 0).reshape(devices * examples_dev, rank * rank)
    stored_rows = stored.shape[0]
    column = position * stored_rows + jnp.arange(stored_rows, dtype=jnp.int32)
    products = lax.dot_general(
        queries, stored, (((1,), (1,)), ((), ())), preferred_element_type=F32
    )
    return jnp.where(column[None, :] < visible[:, None], products, F32(0.0))


def solution(mesh):
    return jax.shard_map(
        shards,
        mesh=mesh,
        in_specs=(
            P(("ckpt", "row"), None),
            P(("ckpt", "row"), None),
            P(("ckpt", "row"), None),
            P(("ckpt", "row"), None),
            P(),
            P(),
            P(("ckpt", "row"), None),
            P(),
        ),
        out_specs=P("ckpt", "row"),
        check_vma=False,
    )
```

```python
import functools

import jax
import jax.numpy as jnp
from jax import lax
from jax.experimental import pallas as pl
from jax.experimental.pallas import tpu as pltpu
from jax.sharding import PartitionSpec as P

SEQ_LEN = 128
LANE_SHIFT = 2
LANES = 4
QUADS = 1 << LANE_SHIFT
BF16, F32 = jnp.bfloat16, jnp.float32
LINK = jnp.bfloat16


EXTRA = 16


def arrange_kernel(piece, where_ref, gate_ref, rows_ref, in_ref, n0, n1, n2, f0, f1, f2, b3, r0, r1, r2):
    lane, side, core = where_ref[0], where_ref[1], where_ref[2]
    wide = 2 * piece
    tokens = gate_ref.shape[0]

    def put(source, target, column, block, first):
        start = pl.multiple_of(block * wide, 128)
        both = source[:, pl.ds(start, wide)]
        if first == 1:
            both = jnp.concatenate([both[:, piece:], both[:, :piece]], axis=1)
        target[: both.shape[0], column : column + wide] = both

    for target in (f1, f2, b3):
        target[tokens:, :] = jnp.zeros((EXTRA, target.shape[1]), target.dtype)
        target[tokens:, : in_ref.shape[1]] = in_ref[...]
    for first in range(2):

        @pl.when(core == first)
        def _():
            for k in range(LANES):
                for far in range(2):
                    block = (lane ^ k) * 2 + (side ^ far)
                    if k == 3:
                        put(gate_ref, b3, far * wide, block, first)
                    else:
                        put(gate_ref, ((n0, n1, n2), (f0, f1, f2))[far][k], 0, block, first)
                    if k == 0:
                        put(rows_ref, r0, far * wide, block, first)
                    elif k < 3 and not far:
                        put(rows_ref, (r1, r2)[k - 1], 0, block, first)


def arrange(gate, rows, in_block, position, piece):
    lane = position >> LANE_SHIFT & LANES - 1
    quad = position & QUADS - 1
    total = gate.shape[1]
    outer = total // (piece * QUADS * LANES)
    mine = total // LANES
    tokens, rank = gate.shape[0], rows.shape[0]
    if outer == 1 and 2 * piece % 128 == 0:
        where = jnp.stack([lane, quad >> 1, quad & 1]).astype(jnp.int32)
        vmem = pl.BlockSpec(memory_space=pltpu.VMEM)
        near, far = (tokens, mine // 2), (tokens + EXTRA, mine // 2)
        shapes = [near] * 4 + [far] * 2 + [(tokens + EXTRA, mine)]
        shapes += [(rank, mine), (rank, mine // 2), (rank, mine // 2)]
        parts = pl.pallas_call(
            functools.partial(arrange_kernel, piece),
            out_shape=[jax.ShapeDtypeStruct(shape, gate.dtype) for shape in shapes],
            in_specs=[pl.BlockSpec(memory_space=pltpu.SMEM), vmem, vmem, vmem],
            out_specs=[vmem] * len(shapes),
            cost_estimate=pl.CostEstimate(
                flops=0, bytes_accessed=4 * gate.size + 4 * rows.size, transcendentals=0
            ),
            compiler_params=pltpu.CompilerParams(vmem_limit_bytes=16 << 20),
        )(where, gate, rows, in_block)
        return parts[:3], parts[3:6], parts[6], parts[7:]

    def block(value, k):
        whole = []
        for w in range(QUADS):
            index = (lane ^ k) * QUADS + (quad ^ w)
            for o in range(outer):
                start = (o * QUADS * LANES + index) * piece
                whole.append(lax.dynamic_slice_in_dim(value, start, piece, axis=1))
        whole = jnp.concatenate(whole, axis=1)
        return whole[:, : mine // 2], whole[:, mine // 2 :], whole

    def extend(value):
        extra = jnp.pad(in_block, ((0, 0), (0, value.shape[1] - in_block.shape[1])))
        return jnp.concatenate([value, extra], axis=0)

    near, far, whole = zip(*[block(gate, k) for k in range(LANES)])
    sides = [block(rows, 0)[2], block(rows, 1)[0], block(rows, 2)[0]]
    return list(near[:3]), [far[0], extend(far[1]), extend(far[2])], extend(whole[3]), sides


def after(value, *others):
    return lax.optimization_barrier((value,) + others)[0]


def call(body, out_shape, in_specs, out_specs, **kwargs):
    return pl.pallas_call(
        body,
        out_shape=out_shape,
        in_specs=in_specs,
        out_specs=out_specs,
        cost_estimate=pl.CostEstimate(flops=1000, bytes_accessed=1000, transcendentals=0),
        **kwargs,
    )


def silu(gate):
    return 0.5 * gate * (1.0 + jnp.tanh(0.5 * gate))


def in_value(refs, k, tokens):
    if k == 0:
        return refs["in"][...]
    source = refs["block"] if k == 3 else refs["far", k]
    width = refs["in"].shape[0] // EXTRA * tokens
    return source[tokens:, :width]


def feature_kernel(slots, blocks, gates, extras, names, *refs):
    out_ref, ups = refs[-2:]
    refs = dict(zip(names, refs))
    tokens = SEQ_LEN * out_ref.shape[1]
    rank = refs["rows"].shape[0]
    for k in range(LANES):
        if "before" in refs and k not in slots:
            out_ref[k] = refs["before"][k]
    for i, k in enumerate(slots):
        start = 0
        for b, width, tops in blocks:
            part, top = tops[k]
            edge = gates[k][0][1].stop - gates[k][0][1].start
            name, cut = gates[k][start >= edge]
            gate = refs[name]
            base = cut.start + start - edge * (start >= edge)
            value = refs[b, part][top : top + tokens, :].astype(F32)
            ups[i * tokens : (i + 1) * tokens, start : start + width] = (
                value * silu(gate[:tokens, base : base + width].astype(F32))
            ).astype(BF16)
            start += width
    total = lax.dot_general(
        refs["rows"][...], ups[...], (((1,), (1,)), ((), ())), preferred_element_type=F32
    )
    totals = [total[:, i * tokens : (i + 1) * tokens] for i in range(len(slots))]
    for j in range(extras):
        side = refs["side", j][...].astype(F32)
        up_grad = refs["back", j][:, side.shape[1] :].astype(F32) * silu(side)
        totals[0] += lax.dot_general(
            refs["beside", j][...],
            up_grad.astype(BF16),
            (((1,), (1,)), ((), ())),
            preferred_element_type=F32,
        )
    for i, k in enumerate(slots):
        for e in range(out_ref.shape[1]):
            cut = slice(e * SEQ_LEN, (e + 1) * SEQ_LEN)
            value = totals[i][:, cut]
            high = value.astype(BF16)
            low = (value - high.astype(F32)).astype(BF16)
            left = in_value(refs, k, tokens)
            if left.shape[0] == EXTRA:
                left = jnp.concatenate(
                    [left[:, j * tokens : (j + 1) * tokens] for j in range(rank // EXTRA)], axis=0
                )
            left = left[:, cut]
            feature = lax.dot_general(
                jnp.concatenate([left, left], axis=1),
                jnp.concatenate([high, low], axis=1),
                (((1,), (1,)), ((), ())),
                preferred_element_type=F32,
            )
            out_ref[k, e] = jnp.concatenate(
                [feature[: rank // 2], feature[rank // 2 :]], axis=1
            ).astype(out_ref.dtype)


def features(slots, blocks, sources, gates, rows, extras=(), before=None):
    names, operands, specs, layout = [], [], [], []
    rank, mine = rows.shape
    tokens = sources["in"].shape[1]
    vmem = pl.BlockSpec(memory_space=pltpu.VMEM)

    def add(name, value):
        names.append(name)
        operands.append(value)

    for b, parts in enumerate(blocks):
        tops, first = {}, 0
        for i, part in enumerate(parts):
            add((b, i), part)
            for k in range(LANES):
                if first <= k * tokens < first + part.shape[0]:
                    tops[k] = (i, k * tokens - first)
            first += part.shape[0]
        layout.append((b, parts[0].shape[1], tops))
    for name, value in sources.items():
        add(name, value)
    add("rows", rows)
    for j, (back, side, beside) in enumerate(extras):
        add(("back", j), back)
        add(("side", j), side)
        add(("beside", j), beside)
    if before is not None:
        add("before", before)
    return call(
        functools.partial(feature_kernel, slots, layout, gates, len(extras), names),
        jax.ShapeDtypeStruct((LANES, tokens // SEQ_LEN, rank // 2, 2 * rank), LINK),
        [vmem] * len(operands),
        vmem,
        scratch_shapes=[pltpu.VMEM((len(slots) * tokens, mine), BF16)],
        compiler_params=pltpu.CompilerParams(vmem_limit_bytes=16 << 20),
    )(*operands)


def hold_kernel(source, target, sem):
    copy = pltpu.make_async_copy(source, target, sem)
    copy.start()
    copy.wait()


def hold(value, limit):
    return call(
        hold_kernel,
        jax.ShapeDtypeStruct(value.shape, value.dtype),
        [pl.BlockSpec(memory_space=pltpu.HBM)],
        pl.BlockSpec(memory_space=pl.ANY),
        scratch_shapes=[pltpu.SemaphoreType.DMA],
        compiler_params=pltpu.CompilerParams(vmem_limit_bytes=limit << 20),
    )(value)


def scale_kernel(own, *refs):
    others, out_ref = refs[:-1], refs[-1]
    width = own.shape[2] * own.shape[3]
    for j in range(LANES):
        total = own[j].astype(F32)
        for k in range(1, LANES):
            total += others[k - 1][j ^ k].astype(F32)
        square = jnp.sum(jnp.sum(total * total, axis=2, keepdims=True), axis=1, keepdims=True)
        out_ref[j] = (total * lax.rsqrt(square / width + 1e-06)).astype(BF16)


def scaled(own, others):
    vmem = pl.BlockSpec(memory_space=pltpu.VMEM)
    return call(
        scale_kernel,
        jax.ShapeDtypeStruct(own.shape, BF16),
        [vmem] * LANES,
        vmem,
        compiler_params=pltpu.CompilerParams(vmem_limit_bytes=4 << 20),
    )(own, *others)


def score_kernel(where_ref, q0, q1, q2, q3, visible_ref, stored_ref, out_ref, rows):
    position = where_ref[0]
    for w, source in enumerate((q0, q1, q2, q3)):
        for k in range(LANES):
            row = k * QUADS + w
            value = source[k, 0].astype(F32)
            for j in range(value.shape[0]):
                rows[row : row + 1, j * 128 : (j + 1) * 128] = value[j : j + 1, :]
    products = lax.dot_general(
        rows[...].astype(BF16),
        stored_ref[...],
        (((1,), (1,)), ((), ())),
        preferred_element_type=F32,
    )
    count = out_ref.shape[1]
    index = lax.broadcasted_iota(jnp.int32, products.shape, 0)
    for bit in (1, 2, 4, 8):
        swapped = jnp.where(
            index & bit != 0,
            pltpu.roll(products, bit, 0),
            pltpu.roll(products, products.shape[0] - bit, 0),
        )
        products = jnp.where(jnp.full(products.shape, position) & bit != 0, swapped, products)
    column = position * count + lax.broadcasted_iota(jnp.int32, products.shape, 1)
    out_ref[...] = jnp.where(column < visible_ref[...], products, 0.0)


def scores(where, queries, visible, stored):
    vmem = pl.BlockSpec(memory_space=pltpu.VMEM)
    examples = LANES * QUADS
    return call(
        score_kernel,
        jax.ShapeDtypeStruct((examples, stored.shape[0]), F32),
        [pl.BlockSpec(memory_space=pltpu.SMEM)] + [vmem] * 6,
        vmem,
        scratch_shapes=[pltpu.VMEM((examples, stored.shape[1]), F32)],
        compiler_params=pltpu.CompilerParams(vmem_limit_bytes=8 << 20),
    )(where, *queries, visible[:, None], stored)


def shards(activations, gate_pre, out_grad, down_weight, proj_in, proj_out, stored, visible):
    devices = lax.axis_size("row")
    position = lax.axis_index("row")
    total_bits = devices.bit_length() - 1
    lane = position >> LANE_SHIFT & LANES - 1
    tokens = out_grad.shape[0]
    rank = proj_in.shape[1]

    def send(value, move):
        pairs = []
        for i in range(devices):
            target = move(i)
            if target is not None:
                pairs.append((i, target))
        return lax.ppermute(value, "row", pairs)

    def flip(bits):
        return lambda i: i ^ bits

    def lane_move(table):
        def move(i):
            to = table.get(i >> LANE_SHIFT & LANES - 1)
            return None if to is None else i & ~((LANES - 1) << LANE_SHIFT) | to << LANE_SHIFT

        return move

    def join(value, other, bit, axis):
        return jnp.where(
            position >> bit & 1 == 1,
            jnp.concatenate([other, value], axis=axis),
            jnp.concatenate([value, other], axis=axis),
        )

    def gather_high(value, axis):
        for bit in range(LANE_SHIFT + 2, total_bits):
            value = join(value, send(value, flip(1 << bit)), bit, axis)
        return value

    middle_swap = lane_move({1: 2, 2: 1})
    to_ends = lane_move({1: 0, 2: 3})
    at_end = (lane == 0) | (lane == LANES - 1)

    own_w = gather_high(down_weight, 0)
    rows = own_w.shape[0]

    tie = lax.optimization_barrier
    grad_a = send(out_grad, flip(1 << LANE_SHIFT))
    grad_b = send(out_grad, middle_swap)
    far_w = send(own_w, flip(2))
    core_w = send(own_w, flip(1))

    width = proj_in.shape[0]
    paired = proj_in.T.reshape(rank // 2, 2, width).transpose(1, 0, 2).reshape(rank, width)
    in_proj = lax.dot_general(
        paired, activations, (((1,), (1,)), ((), ())), preferred_element_type=F32
    ).astype(BF16)
    in_block = in_proj.reshape(rank // EXTRA, EXTRA, tokens).transpose(1, 0, 2)
    in_block = in_block.reshape(EXTRA, rank // EXTRA * tokens)
    near, far, block_3, sides = arrange(
        gate_pre, proj_out.T, in_block, position, down_weight.shape[0]
    )
    grad_a, core_w, near, far, block_3, sides = tie(
        (grad_a, core_w, near, far, block_3, sides)
    )

    def hidden(grads, weight):
        return lax.dot_general(
            grads, weight, (((1,), (1,)), ((), ())), preferred_element_type=F32
        ).astype(BF16)

    def near_hidden(grads):
        return [hidden(grads, w) for w in (own_w, core_w)]

    half = 2 * rows
    grad_c = send(grad_a, middle_swap)
    grad_d = send(after(grad_b, grad_a), to_ends)
    pair = near_hidden(jnp.concatenate([out_grad, grad_a], axis=0))
    slot_1 = [value[tokens:] for value in pair]
    back_1 = send(jnp.concatenate([near[1], *slot_1], axis=1), lane_move({0: 1, 3: 2}))
    grad_c, near, far, block_3, pair = tie((grad_c, near, far, block_3, pair))

    grad_e = send(grad_c, to_ends)
    block_3 = send(after(block_3, grad_d), flip(3 << LANE_SHIFT))
    grad_2 = jnp.where(at_end, grad_d, grad_c)
    slot_2 = near_hidden(grad_2)
    back_2 = send(jnp.concatenate([near[2], *slot_2], axis=1), lane_move({0: 2, 3: 1}))
    early = jnp.concatenate([out_grad, grad_a, grad_2], axis=0)
    far_v = hold(after(far_w, block_3), 16)
    grad_e, back_2, far_v = tie((grad_e, back_2, far_v))
    narrow = at_end & (jnp.max(grad_e[:16, :128].astype(F32)) < jnp.inf)
    block_3, back_1, back_2, far_w, near, far, narrow = tie(
        (block_3, back_1, back_2, far_w, near, far, narrow)
    )
    cross_w = send(far_w, flip(1))
    far_2 = send(far[2], flip(2 << LANE_SHIFT))
    far_1 = send(far[1], flip(1 << LANE_SHIFT))
    grad_3 = jnp.where(at_end, grad_e, grad_b)
    slot_3 = near_hidden(grad_3)
    grads = jnp.concatenate([early, grad_3], axis=0)
    blocks = list(zip(pair, slot_2, slot_3))
    blocks += [(hidden(grads, far_v),), (hidden(grads, cross_w),)]
    low, high = slice(0, half), slice(half, 2 * half)
    extras = [(back, near[j], sides[j]) for j, back in ((1, back_1), (2, back_2))]
    far_1, far_2, blocks = tie((far_1, far_2, blocks))
    own = features(
        (0, 1, 2, 3),
        blocks,
        {
            "near": near[0],
            "far": far[0],
            ("far", 1): far_1,
            ("far", 2): far_2,
            "back1": back_1,
            "back2": back_2,
            "block": block_3,
            "in": in_proj,
        },
        {
            0: (("near", low), ("far", low)),
            1: (("back1", low), (("far", 1), low)),
            2: (("back2", low), (("far", 2), low)),
            3: (("block", low), ("block", high)),
        },
        sides[0],
        extras,
    )
    queries = scaled(own, [send(own, flip(k << LANE_SHIFT)) for k in range(1, LANES)])
    quad = position & QUADS - 1
    everyone = [queries] + [send(queries, flip(q)) for q in range(1, QUADS)]
    if devices == LANES * QUADS and tokens == SEQ_LEN:
        where = position.astype(jnp.int32).reshape(1)
        held = pltpu.with_memory_space_constraint(hold(after(stored, queries), 46), pltpu.VMEM)
        return scores(where, everyone, visible, held)

    examples_dev = tokens // SEQ_LEN
    everyone = jnp.stack(everyone, axis=1).reshape(LANES * QUADS, examples_dev, rank * rank)
    order = jnp.arange(LANES * QUADS)
    order = (order >> LANE_SHIFT ^ lane) * QUADS + (order & QUADS - 1 ^ quad)
    pick = (order[:, None] == jnp.arange(LANES * QUADS)[None, :]).astype(BF16)
    everyone = jnp.einsum("ij,jef->ief", pick, everyone, preferred_element_type=F32).astype(BF16)
    queries = gather_high(everyone, 0).reshape(devices * examples_dev, rank * rank)
    stored_rows = stored.shape[0]
    column = position * stored_rows + jnp.arange(stored_rows, dtype=jnp.int32)
    products = lax.dot_general(
        queries, stored, (((1,), (1,)), ((), ())), preferred_element_type=F32
    )
    return jnp.where(column[None, :] < visible[:, None], products, F32(0.0))


def solution(mesh):
    return jax.shard_map(
        shards,
        mesh=mesh,
        in_specs=(
            P(("ckpt", "row"), None),
            P(("ckpt", "row"), None),
            P(("ckpt", "row"), None),
            P(("ckpt", "row"), None),
            P(),
            P(),
            P(("ckpt", "row"), None),
            P(),
        ),
        out_specs=P("ckpt", "row"),
        check_vma=False,
    )
```
